32 devices in a mesh: seq: 8 (over y, x, core), head: 4 (over z).
Axes of the slice: x: 2, y: 2, z: 4, core: 2. Of those that a mesh axis runs over, the one named last changes fastest.
Arguments:
- out_grad: bfloat16 [2048, 4096], P('seq', 'head'), may hold values from -7.2 to 7.2
- x_in: bfloat16 [2048, 4096], P('seq', 'head'), may hold values from -6 to 6
- b_in: bfloat16 [2048, 128], P('seq'), may hold values from -2.5 to 2.5
- c_in: bfloat16 [2048, 128], P('seq'), may hold values from -2.5 to 2.5
- dt_raw: float32 [64, 2048], P('head', 'seq'), may hold values from -5.1 to -0.7
- dt_bias: float32 [64], P('head'), may hold values from -0.5 to 0.5
- a_log: float32 [64], P('head'), may hold values from -7.5 to 2.2
- d_skip: float32 [64], P('head'), may hold values from 0.5 to 1.5
- states: bfloat16 [8, 4096, 128], P('seq', 'head'), may hold values from -6 to 6
- w_out: bfloat16 [4096, 4096], P('head'), may hold values from -0.09375 to 0.09375
- w_in: bfloat16 [4096, 4096], P(None, 'head'), may hold values from -0.125 to 0.125
Outputs:
- in_grad: bfloat16 [4096, 2048], P('head', 'seq')
- bc_grad: bfloat16 [256, 2048], P('head', 'seq')
- dt_grad: float32 [64, 2048], P('head', 'seq')
- param_grad: float32 [3, 64], P(None, 'head')
The draws below stay inside these ranges and needn't reach their ends.
All inputs are finite; a program needn't handle non-finite values.
Results may differ from the reference program's by a relative error of at most 0.015.
Values may be sent and summed in bfloat16 or wider, within the bound.
A program may use at most 64 MiB of HBM per device.

```python
import jax
import jax.numpy as jnp
from jax import lax

D = 4096
HEADS = 64
HDIM = 64
STATE = 128
SPAN = 256
TOKENS = 2048
INNER = 4096
GROUP_HEADS = 16
N_HEAD = 4


def draw_out_grad(key, part):
    position = jnp.arange(TOKENS, dtype=jnp.float32) / max(TOKENS - 1, 1)
    base_draw = jnp.clip(jax.random.normal(key, (TOKENS, D), jnp.float32), -4.0, 4.0)
    growth = 0.6 * 3.0 ** position
    return (base_draw * growth[:, None]).astype(jnp.bfloat16)


def draw_a_log(key, part):
    key_order, key_slow, key_fast = jax.random.split(jax.random.fold_in(key, 11), 3)
    ranking = jax.random.permutation(key_order, HEADS)
    slow_head = ranking < HEADS // 2
    slow_rate = jax.random.uniform(key_slow, (HEADS,), jnp.float32, 0.3, 1.5) / (TOKENS * 0.06)
    fast_rate = jax.random.uniform(key_fast, (HEADS,), jnp.float32, 0.7, 1.4) * 6.0 / (SPAN * 0.06)
    return jnp.log(jnp.where(slow_head, slow_rate, fast_rate))


def draw_dt_raw(key, part):
    key_jitter, key_block = jax.random.split(jax.random.fold_in(key, 23))
    blocks = TOKENS // SPAN
    offset = jax.random.uniform(key_block, (HEADS, blocks, 1), jnp.float32, -0.7, 0.7)
    jitter = jnp.clip(0.5 * jax.random.normal(key_jitter, (HEADS, blocks, SPAN), jnp.float32), -1.5, 1.5)
    return (-2.9 + offset + jitter).reshape(HEADS, TOKENS)


def strengthened(values, key, source, target, parts, factor):
    def block_of(axis_at):
        return (jnp.arange(values.shape[axis_at]) // (values.shape[axis_at] // parts)).reshape((-1,) + (1,) * (values.ndim - 1 - axis_at))

    near = jax.random.permutation(key, parts)[block_of(target)]
    second = (block_of(target) + parts // 2) % parts
    return jnp.where((block_of(source) == near) | (block_of(source) == second), factor * values, values)


def steps_of(stream_key, extent, cuts, smallest, largest):
    gain, own = 1.0, jax.random.fold_in(stream_key, 6)
    for dim, shards_of in cuts:
        heights = jnp.exp(jax.random.uniform(jax.random.fold_in(own, dim), (shards_of,), jnp.float32, smallest / len(cuts), largest / len(cuts)))
        gain = gain * jnp.repeat(heights, extent[dim] // shards_of).reshape([-1 if axis == dim else 1 for axis in range(len(extent))])
    return gain


def gaussian(stream_key, extent, width, limit, pieces=(), held_as=jnp.bfloat16):
    array = width * jax.random.normal(stream_key, extent, jnp.float32)
    if pieces:
        array = array * steps_of(stream_key, extent, pieces, -0.22, 0.18)
    return jnp.clip(array, -limit, limit).astype(held_as)


def bell_draw_with(stream_key, dims, spread, most, shards, heavy, kind=jnp.bfloat16):
    entries = spread * jax.random.normal(stream_key, dims, jnp.float32)
    if shards:
        entries = entries * steps_of(stream_key, dims, shards, -0.22, 0.18)
    return jnp.clip(strengthened(entries, jax.random.fold_in(stream_key, 3), *heavy), -most, most).astype(kind)


def setup_inputs(seed: int = 0) -> dict:
    key_list = jax.random.split(jax.random.key(seed), 12)
    out_grad = draw_out_grad(jax.random.fold_in(key_list[11], 71), 0)
    x_in = gaussian(key_list[1], (TOKENS, INNER), 1.0, 6.0, ((0, 8), (1, 4)))
    b_in = gaussian(key_list[2], (TOKENS, STATE), 0.3, 2.5, ((0, 8),))
    c_in = gaussian(key_list[3], (TOKENS, STATE), 0.3, 2.5, ((0, 8),))
    dt_raw = draw_dt_raw(jax.random.fold_in(key_list[11], 71), 0)
    dt_bias = jnp.clip(jax.random.uniform(key_list[5], (HEADS,), jnp.float32, -0.5, 0.5) * steps_of(key_list[5], (HEADS,), ((0, 4),), -0.4, 0.0), -0.5, 0.5)
    a_log = draw_a_log(jax.random.fold_in(key_list[11], 71), 0)
    d_skip = jnp.clip(0.5 + 1.0 * jax.random.uniform(key_list[7], (HEADS,), jnp.float32) ** steps_of(key_list[7], (HEADS,), ((0, 4),), -0.2, 0.2), 0.5, 1.5)
    states = gaussian(key_list[8], (TOKENS // SPAN, INNER, STATE), 1.0, 6.0, ((0, 8), (1, 4)))
    w_out = gaussian(key_list[9], (INNER, D), INNER ** -0.5, 0.09375, ((0, 4),))
    w_in = bell_draw_with(key_list[10], (D, INNER), D ** -0.5, 0.125, ((1, 4),), (1, 0, 4, 2.0))
    return dict(out_grad=out_grad, x_in=x_in, b_in=b_in, c_in=c_in, dt_raw=dt_raw, dt_bias=dt_bias, a_log=a_log, d_skip=d_skip, states=states, w_out=w_out, w_in=w_in)


def rounded(values):
    return lax.optimization_barrier(values.astype(jnp.bfloat16)).astype(jnp.float32)


def reference(out_grad, x_in, b_in, c_in, dt_raw, dt_bias, a_log, d_skip, states, w_out, w_in):
    blocks = TOKENS // SPAN
    head_grad = jnp.dot(out_grad, w_out.T, preferred_element_type=jnp.float32).astype(jnp.bfloat16)
    decay_rate = jnp.exp(a_log)
    step_size = jax.nn.softplus(dt_raw + dt_bias[:, None])
    x_blocks = x_in.astype(jnp.float32).reshape(blocks, SPAN, HEADS, HDIM)
    dy_blocks = head_grad.astype(jnp.float32).reshape(blocks, SPAN, HEADS, HDIM)
    b_blocks = b_in.reshape(blocks, SPAN, STATE)
    c_blocks = c_in.reshape(blocks, SPAN, STATE)
    step_blocks = step_size.reshape(HEADS, blocks, SPAN).transpose(1, 0, 2)
    raw_blocks = dt_raw.reshape(HEADS, blocks, SPAN).transpose(1, 0, 2)
    entry_blocks = states.astype(jnp.float32).reshape(blocks, HEADS, HDIM, STATE)
    causal = jnp.arange(SPAN)[:, None] >= jnp.arange(SPAN)[None, :]

    def front(items):
        dy_heads, c_block, step_block = items
        cumlog = jnp.cumsum(-decay_rate[:, None] * step_block, axis=1)
        dy_decay = rounded(dy_heads * jnp.exp(cumlog).T[:, :, None])
        local_state = jnp.einsum('ihp,in->hpn', dy_decay, c_block.astype(jnp.float32))
        return local_state, jnp.exp(cumlog[:, -1])

    local_states, end_totals = lax.map(front, (dy_blocks, c_blocks, step_blocks))

    def carry_step(held_state, items):
        local_state, end_total = items
        return end_total[:, None, None] * held_state + local_state, held_state

    final_state, carried = lax.scan(carry_step, jnp.zeros((HEADS, HDIM, STATE), jnp.float32), (local_states, end_totals), reverse=True)

    def back(items):
        x_heads, dy_heads, b_block, c_block, step_block, raw_block, entry_state, held_state = items
        b_wide = b_block.astype(jnp.float32)
        c_wide = c_block.astype(jnp.float32)
        log_step = -decay_rate[:, None] * step_block
        cumlog = jnp.cumsum(log_step, axis=1)
        log_gaps = cumlog[:, :, None] - cumlog[:, None, :]
        decay_mask = jnp.where(causal[None], jnp.exp(jnp.minimum(log_gaps, 0.0)), 0.0)
        scores = jnp.dot(c_block, b_block.T, preferred_element_type=jnp.float32)
        step_rows = step_block.T
        x_scaled = rounded(x_heads * step_rows[:, :, None])
        pair_dots = jnp.einsum('ihp,jhp->hij', dy_heads, x_scaled)
        kernel = rounded(scores[None] * decay_mask)
        intra_back = jnp.einsum('hij,ihp->jhp', kernel, dy_heads)
        masked_dots = rounded(pair_dots * decay_mask)
        start_decay = jnp.exp(cumlog)
        dy_decay = rounded(dy_heads * start_decay.T[:, :, None])
        carried_bf = rounded(held_state)
        state_back = jnp.einsum('jn,hpn->jhp', b_wide, carried_bf)
        end_decay = jnp.exp(cumlog[:, -1:] - cumlog)
        end_weight = (step_block * end_decay).T
        x_grad = (step_rows[:, :, None] * intra_back + end_weight[:, :, None] * state_back + d_skip[None, :, None] * dy_heads).astype(jnp.bfloat16)
        x_end = rounded(x_heads * end_weight[:, :, None])
        db_heads = jnp.einsum('hij,in->hjn', masked_dots, c_wide) + jnp.einsum('jhp,hpn->hjn', x_end, carried_bf)
        dc_heads = jnp.einsum('hij,jn->hin', masked_dots, b_wide) + jnp.einsum('ihp,hpn->hin', dy_decay, entry_state)
        db_groups = rounded(db_heads.reshape(N_HEAD, GROUP_HEADS, SPAN, STATE).sum(axis=1)).sum(axis=0)
        dc_groups = rounded(dc_heads.reshape(N_HEAD, GROUP_HEADS, SPAN, STATE).sum(axis=1)).sum(axis=0)
        bc_block = jnp.concatenate([db_groups.T, dc_groups.T], axis=0)
        ystate = jnp.einsum('in,hpn->ihp', c_wide, entry_state)
        pair_weight = pair_dots * scores[None] * decay_mask
        state_terms = start_decay * jnp.sum(dy_heads * ystate, axis=2).T
        end_terms = end_weight.T * jnp.sum(x_heads * state_back, axis=2).T
        cum_grad = pair_weight.sum(axis=2) - pair_weight.sum(axis=1) + state_terms - end_terms
        tail_grad = end_terms.sum(axis=1) + jnp.exp(cumlog[:, -1]) * jnp.sum(entry_state * held_state, axis=(1, 2))
        cum_grad = cum_grad.at[:, -1].add(tail_grad)
        step_grad = jnp.cumsum(cum_grad[:, ::-1], axis=1)[:, ::-1]
        dt_sum = -decay_rate[:, None] * step_grad + jnp.sum(x_heads * (intra_back + end_decay.T[:, :, None] * state_back), axis=2).T
        dt_grad = dt_sum * jax.nn.sigmoid(raw_block + dt_bias[:, None])
        param_terms = jnp.stack([jnp.sum(step_grad * log_step, axis=1), jnp.sum(dy_heads * x_heads, axis=(0, 2)), jnp.sum(dt_grad, axis=1)])
        return x_grad, bc_block, dt_grad, param_terms

    x_grads, bc_blocks, dt_blocks, param_blocks = lax.map(back, (x_blocks, dy_blocks, b_blocks, c_blocks, step_blocks, raw_blocks, entry_blocks, carried))
    x_grad = x_grads.reshape(TOKENS, HEADS * HDIM)
    bc_grad = bc_blocks.transpose(1, 0, 2).reshape(2 * STATE, TOKENS).astype(jnp.bfloat16)
    dt_grad = dt_blocks.transpose(1, 0, 2).reshape(HEADS, TOKENS)
    param_grad = param_blocks.sum(axis=0) * (TOKENS * HDIM) ** -0.5
    group_width = GROUP_HEADS * HDIM
    running = jnp.zeros((D, TOKENS), jnp.float32)
    for group_index in range(N_HEAD):
        w_cols = w_in[:, group_index * group_width:(group_index + 1) * group_width]
        x_cols = x_grad[:, group_index * group_width:(group_index + 1) * group_width]
        running = running + rounded(jnp.dot(w_cols, x_cols.T, preferred_element_type=jnp.float32))
    return running.astype(jnp.bfloat16), bc_grad, dt_grad, param_grad
```

```python
import jax
import jax.numpy as jnp
from jax import lax
from jax.sharding import PartitionSpec as P


def partners(count, distance):
    return [(place, place ^ distance) for place in range(count)]


def entering(decay, state, axis):
    count, mine = (lax.axis_size(axis), lax.axis_index(axis))
    carried = jnp.zeros_like(state)
    reach = jnp.ones_like(decay)
    distance = 1
    while distance < count:
        pairs = partners(count, distance)
        other_decay = lax.ppermute(decay, axis, pairs)
        other_state = lax.ppermute(state.astype(jnp.bfloat16), axis, pairs).astype(jnp.float32)
        earlier = (mine // distance) % 2 == 0
        carried = jnp.where(earlier, carried + reach[:, None, None] * other_state, carried)
        reach = jnp.where(earlier, reach * other_decay, reach)
        state = jnp.where(
            earlier,
            state + decay[:, None, None] * other_state,
            other_state + other_decay[:, None, None] * state,
        )
        decay = decay * other_decay
        distance *= 2
    return carried


def summed(value, axis):
    count = lax.axis_size(axis)
    distance = 1
    while distance < count:
        value = value + lax.ppermute(value, axis, partners(count, distance))
        distance *= 2
    return value


def shards(out_grad, x_in, b_in, c_in, dt_raw, dt_bias, a_log, d_skip, states, w_out, w_in):
    tokens_here, inner_here = x_in.shape
    group_heads = dt_raw.shape[0]
    head_dim = inner_here // group_heads
    state_dim = b_in.shape[1]
    contract_last = (((1,), (1,)), ((), ()))
    head_sum = lax.dot_general(
        lax.all_gather(out_grad, "head", axis=1, tiled=True),
        w_out,
        contract_last,
        preferred_element_type=jnp.float32,
    )
    dy_heads = head_sum.astype(jnp.bfloat16).reshape(tokens_here, group_heads, head_dim)
    dy_wide = dy_heads.astype(jnp.float32)
    x_heads = x_in.reshape(tokens_here, group_heads, head_dim)
    x_wide = x_heads.astype(jnp.float32)
    decay_rate = jnp.exp(a_log)
    step_size = jax.nn.softplus(dt_raw + dt_bias[:, None])
    log_step = -decay_rate[:, None] * step_size
    cumlog = jnp.cumsum(log_step, axis=1)
    positions = jnp.arange(tokens_here)
    causal = positions[:, None] >= positions[None, :]
    log_gaps = cumlog[:, :, None] - cumlog[:, None, :]
    decay_mask = jnp.where(causal[None], jnp.exp(jnp.minimum(log_gaps, 0.0)), 0.0)
    scores = lax.dot_general(c_in, b_in, contract_last, preferred_element_type=jnp.float32)
    step_rows = step_size.T
    x_scaled = (x_wide * step_rows[:, :, None]).astype(jnp.bfloat16)
    pair_dots = jnp.einsum("ihp,jhp->hij", dy_heads, x_scaled, preferred_element_type=jnp.float32)
    kernel = (scores[None] * decay_mask).astype(jnp.bfloat16)
    intra_back = jnp.einsum("hij,ihp->jhp", kernel, dy_heads, preferred_element_type=jnp.float32)
    masked_dots = (pair_dots * decay_mask).astype(jnp.bfloat16)
    start_decay = jnp.exp(cumlog)
    dy_decay = (dy_wide * start_decay.T[:, :, None]).astype(jnp.bfloat16)
    local_state = jnp.einsum("ihp,in->hpn", dy_decay, c_in, preferred_element_type=jnp.float32)
    end_total = jnp.exp(cumlog[:, -1])
    entry_state = states.reshape(group_heads, head_dim, state_dim)
    db_intra = jnp.einsum("hij,in->nj", masked_dots, c_in, preferred_element_type=jnp.float32)
    dc_intra = jnp.einsum("hij,jn->ni", masked_dots, b_in, preferred_element_type=jnp.float32)
    dc_entry = jnp.einsum("ihp,hpn->ni", dy_decay, entry_state, preferred_element_type=jnp.float32)
    ystate = jnp.einsum("in,hpn->ihp", c_in, entry_state, preferred_element_type=jnp.float32)
    pair_weight = pair_dots * scores[None] * decay_mask
    state_terms = start_decay * jnp.sum(dy_wide * ystate, axis=2).T
    skip_terms = jnp.sum(dy_wide * x_wide, axis=(0, 2))

    carried = entering(end_total, local_state, "seq")
    carried_bf = carried.astype(jnp.bfloat16)
    state_back = jnp.einsum("jn,hpn->jhp", b_in, carried_bf, preferred_element_type=jnp.float32)
    end_decay = jnp.exp(cumlog[:, -1:] - cumlog)
    end_weight = (step_size * end_decay).T
    x_grad = (
        (
            step_rows[:, :, None] * intra_back
            + end_weight[:, :, None] * state_back
            + d_skip[None, :, None] * dy_wide
        )
        .astype(jnp.bfloat16)
        .reshape(tokens_here, inner_here)
    )
    x_end = (x_wide * end_weight[:, :, None]).astype(jnp.bfloat16)
    db_entry = jnp.einsum("jhp,hpn->nj", x_end, carried_bf, preferred_element_type=jnp.float32)
    bc_part = jnp.concatenate([db_intra + db_entry, dc_intra + dc_entry], axis=0)
    end_terms = end_weight.T * jnp.sum(x_wide * state_back, axis=2).T
    cum_grad = pair_weight.sum(axis=2) - pair_weight.sum(axis=1) + state_terms - end_terms
    tail_grad = end_terms.sum(axis=1) + end_total * jnp.sum(
        entry_state.astype(jnp.float32) * carried, axis=(1, 2)
    )
    cum_grad = cum_grad.at[:, -1].add(tail_grad)
    step_grad = jnp.cumsum(cum_grad[:, ::-1], axis=1)[:, ::-1]
    dt_sum = (
        -decay_rate[:, None] * step_grad
        + jnp.sum(x_wide * (intra_back + end_decay.T[:, :, None] * state_back), axis=2).T
    )
    dt_grad = dt_sum * jax.nn.sigmoid(dt_raw + dt_bias[:, None])
    param_terms = jnp.stack(
        [jnp.sum(step_grad * log_step, axis=1), skip_terms, jnp.sum(dt_grad, axis=1)]
    )
    heads_count = lax.axis_size("head")
    in_term = lax.dot_general(
        w_in, x_grad, contract_last, preferred_element_type=jnp.float32
    ).astype(jnp.bfloat16)
    rows_here = in_term.shape[0] // heads_count
    both = jnp.concatenate(
        [
            in_term.reshape(heads_count, rows_here, tokens_here),
            bc_part.astype(jnp.bfloat16).reshape(heads_count, -1, tokens_here),
        ],
        axis=1,
    )
    both_sum = lax.psum_scatter(
        both.reshape(-1, tokens_here), "head", scatter_dimension=0, tiled=True
    )
    in_part, bc_sum = (both_sum[:rows_here], both_sum[rows_here:])
    norm_scale = (lax.axis_size("seq") * tokens_here * head_dim) ** (-0.5)
    param_grad = summed(param_terms, "seq") * norm_scale
    return (in_part, bc_sum, dt_grad, param_grad)


def solution(mesh):
    return jax.shard_map(
        shards,
        mesh=mesh,
        in_specs=(
            P("seq", "head"),
            P("seq", "head"),
            P("seq", None),
            P("seq", None),
            P("head", "seq"),
            P("head"),
            P("head"),
            P("head"),
            P("seq", "head", None),
            P("head", None),
            P(None, "head"),
        ),
        out_specs=(P("head", "seq"), P("head", "seq"), P("head", "seq"), P(None, "head")),
        check_vma=False,
    )
```

```python
import functools

import jax
import jax.numpy as jnp
from jax import lax
from jax.experimental import pallas as pl
from jax.experimental.pallas import tpu as pltpu
from jax.sharding import PartitionSpec as P


def partners(count, distance):
    return [(place, place ^ distance) for place in range(count)]


def entering(decay, state, axis):
    count, mine = (lax.axis_size(axis), lax.axis_index(axis))
    carried = jnp.zeros_like(state)
    reach = jnp.ones_like(decay)
    distance = 1
    while distance < count:
        pairs = partners(count, distance)
        other_decay = lax.ppermute(decay, axis, pairs)
        other_state = lax.ppermute(state.astype(jnp.bfloat16), axis, pairs).astype(jnp.float32)
        earlier = (mine // distance) % 2 == 0
        carried = jnp.where(earlier, carried + reach[:, None, None] * other_state, carried)
        reach = jnp.where(earlier, reach * other_decay, reach)
        state = jnp.where(
            earlier,
            state + decay[:, None, None] * other_state,
            other_state + other_decay[:, None, None] * state,
        )
        decay = decay * other_decay
        distance *= 2
    return carried


LAST = (((1,), (1,)), ((), ()))
MESH = pl.DeviceIdType.MESH


def tile_of(extent):
    return 256 if extent % 256 == 0 else extent


def ring_copy(src, dst, sems, way, step, target):
    return pltpu.make_async_remote_copy(
        src_ref=src,
        dst_ref=dst,
        send_sem=sems[0].at[way, step],
        recv_sem=sems[1].at[way, step],
        device_id={"head": target},
        device_id_type=MESH,
    )


def gather_matmul_kernel(n, x_ref, w_hbm, o_ref, held, w_ref, total, send_sem, recv_sem, w_sem):
    me = lax.axis_index("head")
    right, left = (lax.rem(me + 1, n), lax.rem(me + n - 1, n))
    tokens, depth = x_ref.shape
    half = tokens // 2
    width = o_ref.shape[1]
    tile = tile_of(width)

    def columns(offset):
        owner = lax.rem(me + offset, n)
        return pl.ds(pl.multiple_of(owner * depth, depth), depth)

    def w_copy(offset):
        where = columns(offset)
        return pltpu.make_async_copy(w_hbm.at[:, where], w_ref.at[:, where], w_sem.at[offset])

    barrier = pltpu.get_barrier_semaphore()
    for neighbour in (left, right):
        pl.semaphore_signal(barrier, inc=1, device_id={"head": neighbour}, device_id_type=MESH)
    pl.semaphore_wait(barrier, 2)
    sems = (send_sem, recv_sem)
    order = []
    for step in range(n):
        for offset in ((n - step) % n, step):
            if offset not in order:
                order.append(offset)
    loaded = set()
    sent = []
    for step in range(n):
        sources = []
        for way, target in ((0, right), (1, left)):
            rows = pl.ds(way * half, half)
            source = x_ref.at[rows] if step == 0 else held.at[step - 1, rows]
            sources.append(source)
            if step > 0:
                sent[2 * (step - 1) + way].wait_recv()
            if step < n - 1:
                copy = ring_copy(source, held.at[step, rows], sems, way, step, target)
                copy.start()
                sent.append(copy)
        if step == 0:
            for offset in order:
                w_copy(offset).start()
        for way in (0, 1):
            offset = (n - step) % n if way == 0 else step
            if offset not in loaded:
                w_copy(offset).wait()
                loaded.add(offset)
            where = columns(offset)
            rows = pl.ds(way * half, half)
            source = sources[way]

            def multiply(index, carry):
                outs = pl.ds(pl.multiple_of(index * tile, tile), tile)
                part = lax.dot_general(
                    source[...], w_ref[outs, where], LAST, preferred_element_type=jnp.float32
                )
                if step > 0:
                    part = part + total[rows, outs]
                if step < n - 1:
                    total[rows, outs] = part
                else:
                    o_ref[rows, outs] = part.astype(o_ref.dtype)
                return carry

            lax.fori_loop(0, width // tile, multiply, 0)
    for copy in sent:
        copy.wait_send()


def gather_matmul(x, w):
    n = lax.axis_size("head")
    tokens, depth = x.shape
    width = w.shape[0]
    vmem = pl.BlockSpec(memory_space=pltpu.VMEM)
    return pl.pallas_call(
        functools.partial(gather_matmul_kernel, n),
        out_shape=jax.ShapeDtypeStruct((tokens, width), jnp.bfloat16),
        in_specs=[vmem, pl.BlockSpec(memory_space=pl.ANY)],
        out_specs=vmem,
        scratch_shapes=[
            pltpu.VMEM((n - 1, tokens, depth), jnp.bfloat16),
            pltpu.VMEM(w.shape, jnp.bfloat16),
            pltpu.VMEM((tokens, width), jnp.float32),
            pltpu.SemaphoreType.DMA((2, n - 1)),
            pltpu.SemaphoreType.DMA((2, n - 1)),
            pltpu.SemaphoreType.DMA((n,)),
        ],
        compiler_params=pltpu.CompilerParams(
            collective_id=0, has_side_effects=True, vmem_limit_bytes=40 * 2**20
        ),
        name="gather_matmul",
    )(x, w)


def matmul_scatter_kernel(
    n, s, w_hbm, x_ref, bc_ref, p_ref, o_ref, obc_ref, op_ref,
    w_ref, going, coming, p_in, send_sem, recv_sem, w_sem, p_send, p_recv,
):
    me = lax.axis_index("head")
    mine = lax.axis_index("seq")
    right, left = (lax.rem(me + 1, n), lax.rem(me + n - 1, n))
    rows_here = o_ref.shape[0]
    half = rows_here // 2
    bc_half = obc_ref.shape[0] // 2
    tile = tile_of(half)

    def owner_of(way, step):
        return lax.rem(me + 2 * n - 1 - step, n) if way == 0 else lax.rem(me + 1 + step, n)

    def w_copy(way, step):
        start = pl.multiple_of(owner_of(way, step) * rows_here + way * half, half)
        rows = pl.ds(start, half)
        return pltpu.make_async_copy(w_hbm.at[rows], w_ref.at[rows], w_sem.at[way, step])

    for step in range(n):
        for way in (0, 1):
            w_copy(way, step).start()
    barrier = pltpu.get_barrier_semaphore()
    for neighbour in (left, right):
        pl.semaphore_signal(barrier, inc=1, device_id={"head": neighbour}, device_id_type=MESH)
    for away in range(1, s):
        pl.semaphore_signal(
            barrier, inc=1, device_id={"seq": lax.rem(mine + away, s)}, device_id_type=MESH
        )
    pl.semaphore_wait(barrier, 2 + s - 1)
    sems = (send_sem, recv_sem)
    p_copies = []
    for away in range(1, s):
        copy = pltpu.make_async_remote_copy(
            src_ref=p_ref,
            dst_ref=p_in.at[away - 1],
            send_sem=p_send.at[away - 1],
            recv_sem=p_recv.at[away - 1],
            device_id={"seq": lax.rem(mine + away, s)},
            device_id_type=MESH,
        )
        p_copies.append(copy)
    sent = []
    for step in range(n):
        now = []
        for way, target in ((0, right), (1, left)):
            owner = owner_of(way, step)
            w_copy(way, step).wait()
            if step > 0:
                sent[2 * (step - 1) + way].wait_recv()
            first = pl.multiple_of(owner * rows_here + way * half, half)

            def finish(start, count, part, target_ref, base):
                if step > 0:
                    old = coming[way, step - 1, pl.ds(start, count), :]
                    part = part.astype(jnp.bfloat16).astype(jnp.float32) + old.astype(jnp.float32)
                if step < n - 1:
                    going[way, step, pl.ds(start, count), :] = part.astype(jnp.bfloat16)
                else:
                    target_ref[pl.ds(base, count), :] = part.astype(jnp.bfloat16)

            def multiply(index, carry):
                start = pl.multiple_of(index * tile, tile)
                part = lax.dot_general(
                    w_ref[pl.ds(first + start, tile), :],
                    x_ref[...],
                    LAST,
                    preferred_element_type=jnp.float32,
                )
                base = pl.multiple_of(way * half + start, tile)
                finish(start, tile, part, o_ref, base)
                return carry

            lax.fori_loop(0, half // tile, multiply, 0)
            bc_start = pl.multiple_of(owner * 2 * bc_half + way * bc_half, bc_half)
            finish(half, bc_half, bc_ref[pl.ds(bc_start, bc_half), :], obc_ref, way * bc_half)
            if step < n - 1:
                copy = ring_copy(
                    going.at[way, step], coming.at[way, step], sems, way, step, target
                )
                copy.start()
                sent.append(copy)
        if step == 0:
            for copy in p_copies:
                copy.start()
    value = p_ref[...]
    for index, copy in enumerate(p_copies):
        copy.wait_recv()
        value = value + p_in[index]
    op_ref[...] = value
    for copy in p_copies + sent:
        copy.wait_send()


def matmul_scatter(w, x, bc, params):
    n, s = (lax.axis_size("head"), lax.axis_size("seq"))
    tokens = x.shape[0]
    rows_here, bc_here = (w.shape[0] // n, bc.shape[0] // n)
    padded = jnp.zeros((8, 128), jnp.float32).at[: params.shape[0], : params.shape[1]].set(params)
    vmem = pl.BlockSpec(memory_space=pltpu.VMEM)
    packet = (2, n - 1, (rows_here + bc_here) // 2, tokens)
    in_sum, bc_sum, param_sum = pl.pallas_call(
        functools.partial(matmul_scatter_kernel, n, s),
        out_shape=(
            jax.ShapeDtypeStruct((rows_here, tokens), jnp.bfloat16),
            jax.ShapeDtypeStruct((bc_here, tokens), jnp.bfloat16),
            jax.ShapeDtypeStruct((8, 128), jnp.float32),
        ),
        in_specs=[pl.BlockSpec(memory_space=pl.ANY), vmem, vmem, vmem],
        out_specs=(vmem, vmem, vmem),
        scratch_shapes=[
            pltpu.VMEM(w.shape, jnp.bfloat16),
            pltpu.VMEM(packet, jnp.bfloat16),
            pltpu.VMEM(packet, jnp.bfloat16),
            pltpu.VMEM((s - 1, 8, 128), jnp.float32),
            pltpu.SemaphoreType.DMA((2, n - 1)),
            pltpu.SemaphoreType.DMA((2, n - 1)),
            pltpu.SemaphoreType.DMA((2, n)),
            pltpu.SemaphoreType.DMA((s - 1,)),
            pltpu.SemaphoreType.DMA((s - 1,)),
        ],
        compiler_params=pltpu.CompilerParams(
            collective_id=1, has_side_effects=True, vmem_limit_bytes=40 * 2**20
        ),
        name="matmul_scatter",
    )(w, x, bc, padded)
    return in_sum, bc_sum, param_sum[: params.shape[0], : params.shape[1]]


def shards(out_grad, x_in, b_in, c_in, dt_raw, dt_bias, a_log, d_skip, states, w_out, w_in):
    tokens_here, inner_here = x_in.shape
    group_heads = dt_raw.shape[0]
    head_dim = inner_here // group_heads
    state_dim = b_in.shape[1]
    contract_last = (((1,), (1,)), ((), ()))
    head_grad = gather_matmul(out_grad, w_out)
    dy_heads = head_grad.reshape(tokens_here, group_heads, head_dim)
    dy_wide = dy_heads.astype(jnp.float32)
    x_heads = x_in.reshape(tokens_here, group_heads, head_dim)
    x_wide = x_heads.astype(jnp.float32)
    decay_rate = jnp.exp(a_log)
    step_size = jax.nn.softplus(dt_raw + dt_bias[:, None])
    log_step = -decay_rate[:, None] * step_size
    cumlog = jnp.cumsum(log_step, axis=1)
    positions = jnp.arange(tokens_here)
    causal = positions[:, None] >= positions[None, :]
    log_gaps = cumlog[:, :, None] - cumlog[:, None, :]
    decay_mask = jnp.where(causal[None], jnp.exp(jnp.minimum(log_gaps, 0.0)), 0.0)
    scores = lax.dot_general(c_in, b_in, contract_last, preferred_element_type=jnp.float32)
    step_rows = step_size.T
    x_scaled = (x_wide * step_rows[:, :, None]).astype(jnp.bfloat16)
    pair_dots = jnp.einsum("ihp,jhp->hij", dy_heads, x_scaled, preferred_element_type=jnp.float32)
    kernel = (scores[None] * decay_mask).astype(jnp.bfloat16)
    intra_back = jnp.einsum("hij,ihp->jhp", kernel, dy_heads, preferred_element_type=jnp.float32)
    masked_dots = (pair_dots * decay_mask).astype(jnp.bfloat16)
    start_decay = jnp.exp(cumlog)
    dy_decay = (dy_wide * start_decay.T[:, :, None]).astype(jnp.bfloat16)
    local_state = jnp.einsum("ihp,in->hpn", dy_decay, c_in, preferred_element_type=jnp.float32)
    end_total = jnp.exp(cumlog[:, -1])
    entry_state = states.reshape(group_heads, head_dim, state_dim)
    db_intra = jnp.einsum("hij,in->nj", masked_dots, c_in, preferred_element_type=jnp.float32)
    dc_intra = jnp.einsum("hij,jn->ni", masked_dots, b_in, preferred_element_type=jnp.float32)
    dc_entry = jnp.einsum("ihp,hpn->ni", dy_decay, entry_state, preferred_element_type=jnp.float32)
    ystate = jnp.einsum("in,hpn->ihp", c_in, entry_state, preferred_element_type=jnp.float32)
    pair_weight = pair_dots * scores[None] * decay_mask
    state_terms = start_decay * jnp.sum(dy_wide * ystate, axis=2).T
    skip_terms = jnp.sum(dy_wide * x_wide, axis=(0, 2))

    carried = entering(end_total, local_state, "seq")
    carried_bf = carried.astype(jnp.bfloat16)
    state_back = jnp.einsum("jn,hpn->jhp", b_in, carried_bf, preferred_element_type=jnp.float32)
    end_decay = jnp.exp(cumlog[:, -1:] - cumlog)
    end_weight = (step_size * end_decay).T
    x_grad = (
        (
            step_rows[:, :, None] * intra_back
            + end_weight[:, :, None] * state_back
            + d_skip[None, :, None] * dy_wide
        )
        .astype(jnp.bfloat16)
        .reshape(tokens_here, inner_here)
    )
    x_end = (x_wide * end_weight[:, :, None]).astype(jnp.bfloat16)
    db_entry = jnp.einsum("jhp,hpn->nj", x_end, carried_bf, preferred_element_type=jnp.float32)
    bc_part = jnp.concatenate([db_intra + db_entry, dc_intra + dc_entry], axis=0)
    end_terms = end_weight.T * jnp.sum(x_wide * state_back, axis=2).T
    cum_grad = pair_weight.sum(axis=2) - pair_weight.sum(axis=1) + state_terms - end_terms
    tail_grad = end_terms.sum(axis=1) + end_total * jnp.sum(
        entry_state.astype(jnp.float32) * carried, axis=(1, 2)
    )
    cum_grad = cum_grad.at[:, -1].add(tail_grad)
    step_grad = jnp.cumsum(cum_grad[:, ::-1], axis=1)[:, ::-1]
    dt_sum = (
        -decay_rate[:, None] * step_grad
        + jnp.sum(x_wide * (intra_back + end_decay.T[:, :, None] * state_back), axis=2).T
    )
    dt_grad = dt_sum * jax.nn.sigmoid(dt_raw + dt_bias[:, None])
    param_terms = jnp.stack(
        [jnp.sum(step_grad * log_step, axis=1), skip_terms, jnp.sum(dt_grad, axis=1)]
    )
    in_part, bc_sum, param_sum = matmul_scatter(w_in, x_grad, bc_part, param_terms)
    norm_scale = (lax.axis_size("seq") * tokens_here * head_dim) ** (-0.5)
    param_grad = param_sum * norm_scale
    return (in_part, bc_sum, dt_grad, param_grad)


def solution(mesh):
    return jax.shard_map(
        shards,
        mesh=mesh,
        in_specs=(
            P("seq", "head"),
            P("seq", "head"),
            P("seq", None),
            P("seq", None),
            P("head", "seq"),
            P("head"),
            P("head"),
            P("head"),
            P("seq", "head", None),
            P("head", None),
            P(None, "head"),
        ),
        out_specs=(P("head", "seq"), P("head", "seq"), P("head", "seq"), P(None, "head")),
        check_vma=False,
    )
```

```python
import functools

import jax
import jax.numpy as jnp
from jax import lax
from jax.experimental import pallas as pl
from jax.experimental.pallas import tpu as pltpu
from jax.sharding import PartitionSpec as P


def partners(count, distance):
    return [(place, place ^ distance) for place in range(count)]


def entering(decay, state, axis):
    count, mine = (lax.axis_size(axis), lax.axis_index(axis))
    carried = jnp.zeros_like(state)
    reach = jnp.ones_like(decay)
    distance = 1
    while distance < count:
        pairs = partners(count, distance)
        other_decay = lax.ppermute(decay, axis, pairs)
        other_state = lax.ppermute(state.astype(jnp.bfloat16), axis, pairs).astype(jnp.float32)
        earlier = (mine // distance) % 2 == 0
        carried = jnp.where(earlier, carried + reach[:, None, None] * other_state, carried)
        reach = jnp.where(earlier, reach * other_decay, reach)
        state = jnp.where(
            earlier,
            state + decay[:, None, None] * other_state,
            other_state + other_decay[:, None, None] * state,
        )
        decay = decay * other_decay
        distance *= 2
    return carried


LAST = (((1,), (1,)), ((), ()))
MESH = pl.DeviceIdType.MESH
CHUNKS = 2


def tile_of(extent):
    return 256 if extent % 256 == 0 else extent


def ring_copy(src, dst, sems, way, step, target):
    return pltpu.make_async_remote_copy(
        src_ref=src,
        dst_ref=dst,
        send_sem=sems[0].at[way, step],
        recv_sem=sems[1].at[way, step],
        device_id={"head": target},
        device_id_type=MESH,
    )


def gather_matmul_kernel(n, x_ref, w_hbm, o_ref, held, w_ref, total, send_sem, recv_sem, w_sem):
    me = lax.axis_index("head")
    right, left = (lax.rem(me + 1, n), lax.rem(me + n - 1, n))
    tokens, depth = x_ref.shape
    half = tokens // 2
    width = o_ref.shape[1]
    tile = tile_of(width)

    def columns(offset):
        owner = lax.rem(me + offset, n)
        return pl.ds(pl.multiple_of(owner * depth, depth), depth)

    def w_copy(offset):
        where = columns(offset)
        return pltpu.make_async_copy(w_hbm.at[:, where], w_ref.at[:, where], w_sem.at[offset])

    barrier = pltpu.get_barrier_semaphore()
    for neighbour in (left, right):
        pl.semaphore_signal(barrier, inc=1, device_id={"head": neighbour}, device_id_type=MESH)
    pl.semaphore_wait(barrier, 2)
    sems = (send_sem, recv_sem)
    order = []
    for step in range(n):
        for offset in ((n - step) % n, step):
            if offset not in order:
                order.append(offset)
    loaded = set()
    sent = {}
    for step in range(n):
        for chunk in range(CHUNKS):
            for way, target in ((0, right), (1, left)):
                lane = way * CHUNKS + chunk
                rows = pl.ds(lane * (half // CHUNKS), half // CHUNKS)
                if step > 0:
                    sent[step - 1, lane].wait_recv()
                if step < n - 1:
                    source = x_ref.at[rows] if step == 0 else held.at[step - 1, rows]
                    copy = ring_copy(source, held.at[step, rows], sems, lane, step, target)
                    copy.start()
                    sent[step, lane] = copy
        if step == 0:
            for offset in order:
                w_copy(offset).start()
        for way in (0, 1):
            offset = (n - step) % n if way == 0 else step
            if offset not in loaded:
                w_copy(offset).wait()
                loaded.add(offset)
            where = columns(offset)
            rows = pl.ds(way * half, half)
            source = x_ref.at[rows] if step == 0 else held.at[step - 1, rows]

            def multiply(index, carry):
                outs = pl.ds(pl.multiple_of(index * tile, tile), tile)
                part = lax.dot_general(
                    source[...], w_ref[outs, where], LAST, preferred_element_type=jnp.float32
                )
                if step > 0:
                    part = part + total[rows, outs]
                if step < n - 1:
                    total[rows, outs] = part
                else:
                    o_ref[rows, outs] = part.astype(o_ref.dtype)
                return carry

            lax.fori_loop(0, width // tile, multiply, 0)
    for copy in sent.values():
        copy.wait_send()


def gather_matmul(x, w):
    n = lax.axis_size("head")
    tokens, depth = x.shape
    width = w.shape[0]
    vmem = pl.BlockSpec(memory_space=pltpu.VMEM)
    return pl.pallas_call(
        functools.partial(gather_matmul_kernel, n),
        out_shape=jax.ShapeDtypeStruct((tokens, width), jnp.bfloat16),
        in_specs=[vmem, pl.BlockSpec(memory_space=pl.ANY)],
        out_specs=vmem,
        scratch_shapes=[
            pltpu.VMEM((n - 1, tokens, depth), jnp.bfloat16),
            pltpu.VMEM(w.shape, jnp.bfloat16),
            pltpu.VMEM((tokens, width), jnp.float32),
            pltpu.SemaphoreType.DMA((2 * CHUNKS, n - 1)),
            pltpu.SemaphoreType.DMA((2 * CHUNKS, n - 1)),
            pltpu.SemaphoreType.DMA((n,)),
        ],
        compiler_params=pltpu.CompilerParams(
            collective_id=0, has_side_effects=True, vmem_limit_bytes=60 * 2**20
        ),
        name="gather_matmul",
    )(x, w)


def matmul_scatter_kernel(
    n, s, w_hbm, x_ref, bc_ref, p_ref, o_ref, obc_ref, op_ref,
    w_ref, going, coming, p_in, send_sem, recv_sem, w_sem, p_send, p_recv,
):
    me = lax.axis_index("head")
    mine = lax.axis_index("seq")
    right, left = (lax.rem(me + 1, n), lax.rem(me + n - 1, n))
    rows_here = o_ref.shape[0]
    half = rows_here // 2
    bc_half = obc_ref.shape[0] // 2
    piece = half // CHUNKS
    tile = tile_of(piece)

    def owner_of(way, step):
        return lax.rem(me + 2 * n - 1 - step, n) if way == 0 else lax.rem(me + 1 + step, n)

    def w_copy(way, step):
        start = pl.multiple_of(owner_of(way, step) * rows_here + way * half, half)
        rows = pl.ds(start, half)
        return pltpu.make_async_copy(w_hbm.at[rows], w_ref.at[rows], w_sem.at[way, step])

    for step in range(n):
        for way in (0, 1):
            w_copy(way, step).start()
    barrier = pltpu.get_barrier_semaphore()
    for neighbour in (left, right):
        pl.semaphore_signal(barrier, inc=1, device_id={"head": neighbour}, device_id_type=MESH)
    for away in range(1, s):
        pl.semaphore_signal(
            barrier, inc=1, device_id={"seq": lax.rem(mine + away, s)}, device_id_type=MESH
        )
    pl.semaphore_wait(barrier, 2 + s - 1)
    sems = (send_sem, recv_sem)
    p_copies = []
    for away in range(1, s):
        copy = pltpu.make_async_remote_copy(
            src_ref=p_ref,
            dst_ref=p_in.at[away - 1],
            send_sem=p_send.at[away - 1],
            recv_sem=p_recv.at[away - 1],
            device_id={"seq": lax.rem(mine + away, s)},
            device_id_type=MESH,
        )
        p_copies.append(copy)
    sent = {}
    for step in range(n):
        for chunk, way in ((c, w) for c in range(CHUNKS) for w in (0, 1)):
            target = left if way else right
            lane = way * CHUNKS + chunk
            owner = owner_of(way, step)
            if chunk == 0:
                w_copy(way, step).wait()
            if step > 0:
                sent[step - 1, lane].wait_recv()
            first = pl.multiple_of(owner * rows_here + way * half, half)

            def finish(start, count, part, target_ref, base):
                if step > 0:
                    old = coming[way, step - 1, pl.ds(start, count), :]
                    part = part.astype(jnp.bfloat16).astype(jnp.float32) + old.astype(jnp.float32)
                if step < n - 1:
                    going[way, step, pl.ds(start, count), :] = part.astype(jnp.bfloat16)
                else:
                    target_ref[pl.ds(base, count), :] = part.astype(jnp.bfloat16)

            def multiply(index, carry):
                start = pl.multiple_of(chunk * piece + index * tile, tile)
                part = lax.dot_general(
                    w_ref[pl.ds(first + start, tile), :],
                    x_ref[...],
                    LAST,
                    preferred_element_type=jnp.float32,
                )
                base = pl.multiple_of(way * half + start, tile)
                finish(start, tile, part, o_ref, base)
                return carry

            lax.fori_loop(0, piece // tile, multiply, 0)
            span = piece
            if chunk == CHUNKS - 1:
                span = piece + bc_half
                bc_start = pl.multiple_of(owner * 2 * bc_half + way * bc_half, bc_half)
                finish(half, bc_half, bc_ref[pl.ds(bc_start, bc_half), :], obc_ref, way * bc_half)
            if step < n - 1:
                rows = pl.ds(chunk * piece, span)
                copy = ring_copy(
                    going.at[way, step, rows], coming.at[way, step, rows], sems, lane, step, target
                )
                copy.start()
                sent[step, lane] = copy
        if step == 0:
            for copy in p_copies:
                copy.start()
    value = p_ref[...]
    for index, copy in enumerate(p_copies):
        copy.wait_recv()
        value = value + p_in[index]
    op_ref[...] = value
    for copy in p_copies + list(sent.values()):
        copy.wait_send()


def matmul_scatter(w, x, bc, params):
    n, s = (lax.axis_size("head"), lax.axis_size("seq"))
    tokens = x.shape[0]
    rows_here, bc_here = (w.shape[0] // n, bc.shape[0] // n)
    padded = jnp.zeros((8, 128), jnp.float32).at[: params.shape[0], : params.shape[1]].set(params)
    vmem = pl.BlockSpec(memory_space=pltpu.VMEM)
    packet = (2, n - 1, (rows_here + bc_here) // 2, tokens)
    in_sum, bc_sum, param_sum = pl.pallas_call(
        functools.partial(matmul_scatter_kernel, n, s),
        out_shape=(
            jax.ShapeDtypeStruct((rows_here, tokens), jnp.bfloat16),
            jax.ShapeDtypeStruct((bc_here, tokens), jnp.bfloat16),
            jax.ShapeDtypeStruct((8, 128), jnp.float32),
        ),
        in_specs=[pl.BlockSpec(memory_space=pl.ANY), vmem, vmem, vmem],
        out_specs=(vmem, vmem, vmem),
        scratch_shapes=[
            pltpu.VMEM(w.shape, jnp.bfloat16),
            pltpu.VMEM(packet, jnp.bfloat16),
            pltpu.VMEM(packet, jnp.bfloat16),
            pltpu.VMEM((s - 1, 8, 128), jnp.float32),
            pltpu.SemaphoreType.DMA((2 * CHUNKS, n - 1)),
            pltpu.SemaphoreType.DMA((2 * CHUNKS, n - 1)),
            pltpu.SemaphoreType.DMA((2, n)),
            pltpu.SemaphoreType.DMA((s - 1,)),
            pltpu.SemaphoreType.DMA((s - 1,)),
        ],
        compiler_params=pltpu.CompilerParams(
            collective_id=1, has_side_effects=True, vmem_limit_bytes=60 * 2**20
        ),
        name="matmul_scatter",
    )(w, x, bc, padded)
    return in_sum, bc_sum, param_sum[: params.shape[0], : params.shape[1]]


def shards(out_grad, x_in, b_in, c_in, dt_raw, dt_bias, a_log, d_skip, states, w_out, w_in):
    tokens_here, inner_here = x_in.shape
    group_heads = dt_raw.shape[0]
    head_dim = inner_here // group_heads
    state_dim = b_in.shape[1]
    contract_last = (((1,), (1,)), ((), ()))
    head_grad = gather_matmul(out_grad, w_out)
    dy_heads = head_grad.reshape(tokens_here, group_heads, head_dim)
    x_heads = x_in.reshape(tokens_here, group_heads, head_dim)
    x_wide = x_heads.astype(jnp.float32)
    decay_rate = jnp.exp(a_log)
    step_size = jax.nn.softplus(dt_raw + dt_bias[:, None])
    log_step = -decay_rate[:, None] * step_size
    cumlog = jnp.cumsum(log_step, axis=1)
    positions = jnp.arange(tokens_here)
    causal = positions[:, None] >= positions[None, :]
    log_gaps = cumlog[:, :, None] - cumlog[:, None, :]
    decay_mask = jnp.where(causal[None], jnp.exp(jnp.minimum(log_gaps, 0.0)), 0.0)
    start_decay = jnp.exp(cumlog)
    dy_decay = (dy_heads.astype(jnp.float32) * start_decay.T[:, :, None]).astype(jnp.bfloat16)
    local_state = jnp.einsum("ihp,in->hpn", dy_decay, c_in, preferred_element_type=jnp.float32)
    dy_heads, local_state = lax.optimization_barrier((dy_heads, local_state))
    dy_wide = dy_heads.astype(jnp.float32)
    scores = lax.dot_general(c_in, b_in, contract_last, preferred_element_type=jnp.float32)
    step_rows = step_size.T
    x_scaled = (x_wide * step_rows[:, :, None]).astype(jnp.bfloat16)
    pair_dots = jnp.einsum("ihp,jhp->hij", dy_heads, x_scaled, preferred_element_type=jnp.float32)
    kernel = (scores[None] * decay_mask).astype(jnp.bfloat16)
    intra_back = jnp.einsum("hij,ihp->jhp", kernel, dy_heads, preferred_element_type=jnp.float32)
    masked_dots = (pair_dots * decay_mask).astype(jnp.bfloat16)
    end_total = jnp.exp(cumlog[:, -1])
    entry_state = states.reshape(group_heads, head_dim, state_dim)
    db_intra = jnp.einsum("hij,in->nj", masked_dots, c_in, preferred_element_type=jnp.float32)
    dc_intra = jnp.einsum("hij,jn->ni", masked_dots, b_in, preferred_element_type=jnp.float32)
    dc_entry = jnp.einsum("ihp,hpn->ni", dy_decay, entry_state, preferred_element_type=jnp.float32)
    ystate = jnp.einsum("in,hpn->ihp", c_in, entry_state, preferred_element_type=jnp.float32)
    pair_weight = pair_dots * scores[None] * decay_mask
    state_terms = start_decay * jnp.sum(dy_wide * ystate, axis=2).T
    skip_terms = jnp.sum(dy_wide * x_wide, axis=(0, 2))

    carried = entering(end_total, local_state, "seq")
    carried_bf = carried.astype(jnp.bfloat16)
    state_back = jnp.einsum("jn,hpn->jhp", b_in, carried_bf, preferred_element_type=jnp.float32)
    end_decay = jnp.exp(cumlog[:, -1:] - cumlog)
    end_weight = (step_size * end_decay).T
    x_grad = (
        (
            step_rows[:, :, None] * intra_back
            + end_weight[:, :, None] * state_back
            + d_skip[None, :, None] * dy_wide
        )
        .astype(jnp.bfloat16)
        .reshape(tokens_here, inner_here)
    )
    x_end = (x_wide * end_weight[:, :, None]).astype(jnp.bfloat16)
    db_entry = jnp.einsum("jhp,hpn->nj", x_end, carried_bf, preferred_element_type=jnp.float32)
    bc_part = jnp.concatenate([db_intra + db_entry, dc_intra + dc_entry], axis=0)
    end_terms = end_weight.T * jnp.sum(x_wide * state_back, axis=2).T
    cum_grad = pair_weight.sum(axis=2) - pair_weight.sum(axis=1) + state_terms - end_terms
    tail_grad = end_terms.sum(axis=1) + end_total * jnp.sum(
        entry_state.astype(jnp.float32) * carried, axis=(1, 2)
    )
    cum_grad = cum_grad.at[:, -1].add(tail_grad)
    step_grad = jnp.cumsum(cum_grad[:, ::-1], axis=1)[:, ::-1]
    dt_sum = (
        -decay_rate[:, None] * step_grad
        + jnp.sum(x_wide * (intra_back + end_decay.T[:, :, None] * state_back), axis=2).T
    )
    dt_grad = dt_sum * jax.nn.sigmoid(dt_raw + dt_bias[:, None])
    param_terms = jnp.stack(
        [jnp.sum(step_grad * log_step, axis=1), skip_terms, jnp.sum(dt_grad, axis=1)]
    )
    in_part, bc_sum, param_sum = matmul_scatter(w_in, x_grad, bc_part, param_terms)
    norm_scale = (lax.axis_size("seq") * tokens_here * head_dim) ** (-0.5)
    param_grad = param_sum * norm_scale
    return (in_part, bc_sum, dt_grad, param_grad)


def solution(mesh):
    return jax.shard_map(
        shards,
        mesh=mesh,
        in_specs=(
            P("seq", "head"),
            P("seq", "head"),
            P("seq", None),
            P("seq", None),
            P("head", "seq"),
            P("head"),
            P("head"),
            P("head"),
            P("seq", "head", None),
            P("head", None),
            P(None, "head"),
        ),
        out_specs=(P("head", "seq"), P("head", "seq"), P("head", "seq"), P(None, "head")),
        check_vma=False,
    )
```

```python
import functools

import jax
import jax.numpy as jnp
from jax import lax
from jax.experimental import pallas as pl
from jax.experimental.pallas import tpu as pltpu
from jax.sharding import PartitionSpec as P


def partners(count, distance):
    return [(place, place ^ distance) for place in range(count)]


def entering(decay, state, axis, beside):
    count, mine = (lax.axis_size(axis), lax.axis_index(axis))
    carried = jnp.zeros_like(state)
    reach = jnp.ones_like(decay)
    distance = 1
    while distance < count:
        pairs = partners(count, distance)
        other_decay = lax.ppermute(decay, axis, pairs)
        other_state = lax.ppermute(state.astype(jnp.bfloat16), axis, pairs)
        if distance == 1:
            other_state, beside = lax.optimization_barrier((other_state, beside))
        other_state = other_state.astype(jnp.float32)
        earlier = (mine // distance) % 2 == 0
        carried = jnp.where(earlier, carried + reach[:, None, None] * other_state, carried)
        reach = jnp.where(earlier, reach * other_decay, reach)
        state = jnp.where(
            earlier,
            state + decay[:, None, None] * other_state,
            other_state + other_decay[:, None, None] * state,
        )
        decay = decay * other_decay
        distance *= 2
    return carried, beside


LAST = (((1,), (1,)), ((), ()))
MESH = pl.DeviceIdType.MESH
CHUNKS = 2


def tile_of(extent):
    return 256 if extent % 256 == 0 else extent


def ring_copy(src, dst, sems, way, step, target):
    return pltpu.make_async_remote_copy(
        src_ref=src,
        dst_ref=dst,
        send_sem=sems[0].at[way, step],
        recv_sem=sems[1].at[way, step],
        device_id={"head": target},
        device_id_type=MESH,
    )


def gather_matmul_kernel(n, x_ref, w_hbm, o_ref, held, w_ref, total, send_sem, recv_sem, w_sem):
    me = lax.axis_index("head")
    right, left = (lax.rem(me + 1, n), lax.rem(me + n - 1, n))
    tokens, depth = x_ref.shape
    half = tokens // 2
    width = o_ref.shape[1]
    tile = tile_of(width)

    def columns(offset):
        owner = lax.rem(me + offset, n)
        return pl.ds(pl.multiple_of(owner * depth, depth), depth)

    def w_copy(offset):
        where = columns(offset)
        return pltpu.make_async_copy(w_hbm.at[:, where], w_ref.at[:, where], w_sem.at[offset])

    barrier = pltpu.get_barrier_semaphore()
    for neighbour in (left, right):
        pl.semaphore_signal(barrier, inc=1, device_id={"head": neighbour}, device_id_type=MESH)
    pl.semaphore_wait(barrier, 2)
    sems = (send_sem, recv_sem)
    order = []
    for step in range(n):
        for offset in ((n - step) % n, step):
            if offset not in order:
                order.append(offset)
    loaded = set()
    sent = {}
    for step in range(n):
        for chunk in range(CHUNKS):
            for way, target in ((0, right), (1, left)):
                lane = way * CHUNKS + chunk
                rows = pl.ds(lane * (half // CHUNKS), half // CHUNKS)
                if step > 0:
                    sent[step - 1, lane].wait_recv()
                if step < n - 1:
                    source = x_ref.at[rows] if step == 0 else held.at[step - 1, rows]
                    copy = ring_copy(source, held.at[step, rows], sems, lane, step, target)
                    copy.start()
                    sent[step, lane] = copy
        if step == 0:
            for offset in order:
                w_copy(offset).start()
        for way in (0, 1):
            offset = (n - step) % n if way == 0 else step
            if offset not in loaded:
                w_copy(offset).wait()
                loaded.add(offset)
            where = columns(offset)
            rows = pl.ds(way * half, half)
            source = x_ref.at[rows] if step == 0 else held.at[step - 1, rows]

            def multiply(index, carry):
                outs = pl.ds(pl.multiple_of(index * tile, tile), tile)
                part = lax.dot_general(
                    source[...], w_ref[outs, where], LAST, preferred_element_type=jnp.float32
                )
                if step > 0:
                    part = part + total[rows, outs]
                if step < n - 1:
                    total[rows, outs] = part
                else:
                    o_ref[rows, outs] = part.astype(o_ref.dtype)
                return carry

            lax.fori_loop(0, width // tile, multiply, 0)
    for copy in sent.values():
        copy.wait_send()


def gather_matmul(x, w):
    n = lax.axis_size("head")
    tokens, depth = x.shape
    width = w.shape[0]
    vmem = pl.BlockSpec(memory_space=pltpu.VMEM)
    return pl.pallas_call(
        functools.partial(gather_matmul_kernel, n),
        out_shape=jax.ShapeDtypeStruct((tokens, width), jnp.bfloat16),
        in_specs=[vmem, pl.BlockSpec(memory_space=pltpu.HBM)],
        out_specs=vmem,
        scratch_shapes=[
            pltpu.VMEM((n - 1, tokens, depth), jnp.bfloat16),
            pltpu.VMEM(w.shape, jnp.bfloat16),
            pltpu.VMEM((tokens, width), jnp.float32),
            pltpu.SemaphoreType.DMA((2 * CHUNKS, n - 1)),
            pltpu.SemaphoreType.DMA((2 * CHUNKS, n - 1)),
            pltpu.SemaphoreType.DMA((n,)),
        ],
        compiler_params=pltpu.CompilerParams(
            collective_id=0, has_side_effects=True, vmem_limit_bytes=52 * 2**20
        ),
        name="gather_matmul",
    )(x, w)


def matmul_scatter_kernel(
    n, s, w_hbm, x_ref, bc_ref, p_ref, o_ref, obc_ref, op_ref,
    w_ref, going, coming, p_in, send_sem, recv_sem, w_sem, p_send, p_recv,
):
    me = lax.axis_index("head")
    mine = lax.axis_index("seq")
    right, left = (lax.rem(me + 1, n), lax.rem(me + n - 1, n))
    rows_here = o_ref.shape[0]
    half = rows_here // 2
    bc_half = obc_ref.shape[0] // 2
    piece = half // CHUNKS
    tile = tile_of(piece)

    def owner_of(way, step):
        return lax.rem(me + 2 * n - 1 - step, n) if way == 0 else lax.rem(me + 1 + step, n)

    def w_copy(way, step):
        start = pl.multiple_of(owner_of(way, step) * rows_here + way * half, half)
        rows = pl.ds(start, half)
        return pltpu.make_async_copy(w_hbm.at[rows], w_ref.at[rows], w_sem.at[way, step])

    for step in range(n):
        for way in (0, 1):
            w_copy(way, step).start()
    barrier = pltpu.get_barrier_semaphore()
    for neighbour in (left, right):
        pl.semaphore_signal(barrier, inc=1, device_id={"head": neighbour}, device_id_type=MESH)
    for away in range(1, s):
        pl.semaphore_signal(
            barrier, inc=1, device_id={"seq": lax.rem(mine + away, s)}, device_id_type=MESH
        )
    pl.semaphore_wait(barrier, 2 + s - 1)
    sems = (send_sem, recv_sem)
    p_copies = []
    for away in range(1, s):
        copy = pltpu.make_async_remote_copy(
            src_ref=p_ref,
            dst_ref=p_in.at[away - 1],
            send_sem=p_send.at[away - 1],
            recv_sem=p_recv.at[away - 1],
            device_id={"seq": lax.rem(mine + away, s)},
            device_id_type=MESH,
        )
        p_copies.append(copy)
    sent = {}
    for step in range(n):
        for chunk, way in ((c, w) for c in range(CHUNKS) for w in (0, 1)):
            target = left if way else right
            lane = way * CHUNKS + chunk
            owner = owner_of(way, step)
            if chunk == 0:
                w_copy(way, step).wait()
            if step > 0:
                sent[step - 1, lane].wait_recv()
            first = pl.multiple_of(owner * rows_here + way * half, half)

            def finish(start, count, part, target_ref, base):
                if step > 0:
                    old = coming[way, step - 1, pl.ds(start, count), :]
                    part = part.astype(jnp.bfloat16).astype(jnp.float32) + old.astype(jnp.float32)
                if step < n - 1:
                    going[way, step, pl.ds(start, count), :] = part.astype(jnp.bfloat16)
                else:
                    target_ref[pl.ds(base, count), :] = part.astype(jnp.bfloat16)

            def multiply(index, carry):
                start = pl.multiple_of(chunk * piece + index * tile, tile)
                part = lax.dot_general(
                    w_ref[pl.ds(first + start, tile), :],
                    x_ref[...],
                    LAST,
                    preferred_element_type=jnp.float32,
                )
                base = pl.multiple_of(way * half + start, tile)
                finish(start, tile, part, o_ref, base)
                return carry

            lax.fori_loop(0, piece // tile, multiply, 0)
            span = piece
            if chunk == CHUNKS - 1:
                span = piece + bc_half
                bc_start = pl.multiple_of(owner * 2 * bc_half + way * bc_half, bc_half)
                finish(half, bc_half, bc_ref[pl.ds(bc_start, bc_half), :], obc_ref, way * bc_half)
            if step < n - 1:
                rows = pl.ds(chunk * piece, span)
                copy = ring_copy(
                    going.at[way, step, rows], coming.at[way, step, rows], sems, lane, step, target
                )
                copy.start()
                sent[step, lane] = copy
        if step == 0:
            for copy in p_copies:
                copy.start()
    value = p_ref[...]
    for index, copy in enumerate(p_copies):
        copy.wait_recv()
        value = value + p_in[index]
    op_ref[...] = value
    for copy in p_copies + list(sent.values()):
        copy.wait_send()


def matmul_scatter(w, x, bc, params):
    n, s = (lax.axis_size("head"), lax.axis_size("seq"))
    tokens = x.shape[0]
    rows_here, bc_here = (w.shape[0] // n, bc.shape[0] // n)
    padded = jnp.zeros((8, 128), jnp.float32).at[: params.shape[0], : params.shape[1]].set(params)
    vmem = pl.BlockSpec(memory_space=pltpu.VMEM)
    packet = (2, n - 1, (rows_here + bc_here) // 2, tokens)
    in_sum, bc_sum, param_sum = pl.pallas_call(
        functools.partial(matmul_scatter_kernel, n, s),
        out_shape=(
            jax.ShapeDtypeStruct((rows_here, tokens), jnp.bfloat16),
            jax.ShapeDtypeStruct((bc_here, tokens), jnp.bfloat16),
            jax.ShapeDtypeStruct((8, 128), jnp.float32),
        ),
        in_specs=[pl.BlockSpec(memory_space=pltpu.HBM), vmem, vmem, vmem],
        out_specs=(vmem, vmem, vmem),
        scratch_shapes=[
            pltpu.VMEM(w.shape, jnp.bfloat16),
            pltpu.VMEM(packet, jnp.bfloat16),
            pltpu.VMEM(packet, jnp.bfloat16),
            pltpu.VMEM((s - 1, 8, 128), jnp.float32),
            pltpu.SemaphoreType.DMA((2 * CHUNKS, n - 1)),
            pltpu.SemaphoreType.DMA((2 * CHUNKS, n - 1)),
            pltpu.SemaphoreType.DMA((2, n)),
            pltpu.SemaphoreType.DMA((s - 1,)),
            pltpu.SemaphoreType.DMA((s - 1,)),
        ],
        compiler_params=pltpu.CompilerParams(
            collective_id=1, has_side_effects=True, vmem_limit_bytes=52 * 2**20
        ),
        name="matmul_scatter",
    )(w, x, bc, padded)
    return in_sum, bc_sum, param_sum[: params.shape[0], : params.shape[1]]


def shards(out_grad, x_in, b_in, c_in, dt_raw, dt_bias, a_log, d_skip, states, w_out, w_in):
    tokens_here, inner_here = x_in.shape
    group_heads = dt_raw.shape[0]
    head_dim = inner_here // group_heads
    state_dim = b_in.shape[1]
    contract_last = (((1,), (1,)), ((), ()))
    head_grad = gather_matmul(out_grad, w_out)
    dy_heads = head_grad.reshape(tokens_here, group_heads, head_dim)
    x_heads = x_in.reshape(tokens_here, group_heads, head_dim)
    x_wide = x_heads.astype(jnp.float32)
    decay_rate = jnp.exp(a_log)
    step_size = jax.nn.softplus(dt_raw + dt_bias[:, None])
    log_step = -decay_rate[:, None] * step_size
    cumlog = jnp.cumsum(log_step, axis=1)
    positions = jnp.arange(tokens_here)
    causal = positions[:, None] >= positions[None, :]
    log_gaps = cumlog[:, :, None] - cumlog[:, None, :]
    decay_mask = jnp.where(causal[None], jnp.exp(jnp.minimum(log_gaps, 0.0)), 0.0)
    start_decay = jnp.exp(cumlog)
    dy_decay = (dy_heads.astype(jnp.float32) * start_decay.T[:, :, None]).astype(jnp.bfloat16)
    local_state = jnp.einsum("ihp,in->hpn", dy_decay, c_in, preferred_element_type=jnp.float32)
    end_total = jnp.exp(cumlog[:, -1])
    carried, dy_heads = entering(end_total, local_state, "seq", dy_heads)
    dy_wide = dy_heads.astype(jnp.float32)
    scores = lax.dot_general(c_in, b_in, contract_last, preferred_element_type=jnp.float32)
    step_rows = step_size.T
    x_scaled = (x_wide * step_rows[:, :, None]).astype(jnp.bfloat16)
    pair_dots = jnp.einsum("ihp,jhp->hij", dy_heads, x_scaled, preferred_element_type=jnp.float32)
    kernel = (scores[None] * decay_mask).astype(jnp.bfloat16)
    intra_back = jnp.einsum("hij,ihp->jhp", kernel, dy_heads, preferred_element_type=jnp.float32)
    masked_dots = (pair_dots * decay_mask).astype(jnp.bfloat16)
    entry_state = states.reshape(group_heads, head_dim, state_dim)
    db_intra = jnp.einsum("hij,in->nj", masked_dots, c_in, preferred_element_type=jnp.float32)
    dc_intra = jnp.einsum("hij,jn->ni", masked_dots, b_in, preferred_element_type=jnp.float32)
    dc_entry = jnp.einsum("ihp,hpn->ni", dy_decay, entry_state, preferred_element_type=jnp.float32)
    ystate = jnp.einsum("in,hpn->ihp", c_in, entry_state, preferred_element_type=jnp.float32)
    pair_weight = pair_dots * scores[None] * decay_mask
    state_terms = start_decay * jnp.sum(dy_wide * ystate, axis=2).T
    skip_terms = jnp.sum(dy_wide * x_wide, axis=(0, 2))

    carried_bf = carried.astype(jnp.bfloat16)
    state_back = jnp.einsum("jn,hpn->jhp", b_in, carried_bf, preferred_element_type=jnp.float32)
    end_decay = jnp.exp(cumlog[:, -1:] - cumlog)
    end_weight = (step_size * end_decay).T
    x_grad = (
        (
            step_rows[:, :, None] * intra_back
            + end_weight[:, :, None] * state_back
            + d_skip[None, :, None] * dy_wide
        )
        .astype(jnp.bfloat16)
        .reshape(tokens_here, inner_here)
    )
    x_end = (x_wide * end_weight[:, :, None]).astype(jnp.bfloat16)
    db_entry = jnp.einsum("jhp,hpn->nj", x_end, carried_bf, preferred_element_type=jnp.float32)
    bc_part = jnp.concatenate([db_intra + db_entry, dc_intra + dc_entry], axis=0)
    end_terms = end_weight.T * jnp.sum(x_wide * state_back, axis=2).T
    cum_grad = pair_weight.sum(axis=2) - pair_weight.sum(axis=1) + state_terms - end_terms
    tail_grad = end_terms.sum(axis=1) + end_total * jnp.sum(
        entry_state.astype(jnp.float32) * carried, axis=(1, 2)
    )
    cum_grad = cum_grad.at[:, -1].add(tail_grad)
    step_grad = jnp.cumsum(cum_grad[:, ::-1], axis=1)[:, ::-1]
    dt_sum = (
        -decay_rate[:, None] * step_grad
        + jnp.sum(x_wide * (intra_back + end_decay.T[:, :, None] * state_back), axis=2).T
    )
    dt_grad = dt_sum * jax.nn.sigmoid(dt_raw + dt_bias[:, None])
    param_terms = jnp.stack(
        [jnp.sum(step_grad * log_step, axis=1), skip_terms, jnp.sum(dt_grad, axis=1)]
    )
    in_part, bc_sum, param_sum = matmul_scatter(w_in, x_grad, bc_part, param_terms)
    norm_scale = (lax.axis_size("seq") * tokens_here * head_dim) ** (-0.5)
    param_grad = param_sum * norm_scale
    return (in_part, bc_sum, dt_grad, param_grad)


def solution(mesh):
    return jax.shard_map(
        shards,
        mesh=mesh,
        in_specs=(
            P("seq", "head"),
            P("seq", "head"),
            P("seq", None),
            P("seq", None),
            P("head", "seq"),
            P("head"),
            P("head"),
            P("head"),
            P("seq", "head", None),
            P("head", None),
            P(None, "head"),
        ),
        out_specs=(P("head", "seq"), P("head", "seq"), P("head", "seq"), P(None, "head")),
        check_vma=False,
    )
```

```python
import functools

import jax
import jax.numpy as jnp
from jax import lax
from jax.experimental import pallas as pl
from jax.experimental.pallas import tpu as pltpu
from jax.sharding import PartitionSpec as P


def partners(count, distance):
    return [(place, place ^ distance) for place in range(count)]


def entering(decay, state, axis, beside):
    count, mine = (lax.axis_size(axis), lax.axis_index(axis))
    carried = jnp.zeros_like(state)
    reach = jnp.ones_like(decay)
    distance = 1
    while distance < count:
        pairs = partners(count, distance)
        other_decay = lax.ppermute(decay, axis, pairs)
        other_state = lax.ppermute(state.astype(jnp.bfloat16), axis, pairs)
        if distance == 1:
            other_state, beside = lax.optimization_barrier((other_state, beside))
        other_state = other_state.astype(jnp.float32)
        earlier = (mine // distance) % 2 == 0
        carried = jnp.where(earlier, carried + reach[:, None, None] * other_state, carried)
        reach = jnp.where(earlier, reach * other_decay, reach)
        state = jnp.where(
            earlier,
            state + decay[:, None, None] * other_state,
            other_state + other_decay[:, None, None] * state,
        )
        decay = decay * other_decay
        distance *= 2
    return carried, beside


LAST = (((1,), (1,)), ((), ()))
MESH = pl.DeviceIdType.MESH
CHUNKS = 4


def tile_of(extent):
    return 256 if extent % 256 == 0 else extent


def ring_copy(src, dst, sems, way, step, target):
    return pltpu.make_async_remote_copy(
        src_ref=src,
        dst_ref=dst,
        send_sem=sems[0].at[way, step],
        recv_sem=sems[1].at[way, step],
        device_id={"head": target},
        device_id_type=MESH,
    )


def gather_matmul_kernel(n, x_ref, w_hbm, o_ref, held, w_ref, total, send_sem, recv_sem, w_sem):
    me = lax.axis_index("head")
    right, left = (lax.rem(me + 1, n), lax.rem(me + n - 1, n))
    tokens, depth = x_ref.shape
    half = tokens // 2
    width = o_ref.shape[1]
    tile = tile_of(width)

    def columns(offset):
        owner = lax.rem(me + offset, n)
        return pl.ds(pl.multiple_of(owner * depth, depth), depth)

    def w_copy(offset):
        where = columns(offset)
        return pltpu.make_async_copy(w_hbm.at[:, where], w_ref.at[:, where], w_sem.at[offset])

    barrier = pltpu.get_barrier_semaphore()
    for neighbour in (left, right):
        pl.semaphore_signal(barrier, inc=1, device_id={"head": neighbour}, device_id_type=MESH)
    pl.semaphore_wait(barrier, 2)
    sems = (send_sem, recv_sem)
    order = []
    for step in range(n):
        for offset in ((n - step) % n, step):
            if offset not in order:
                order.append(offset)
    loaded = set()
    sent = {}
    for step in range(n):
        for chunk in range(CHUNKS):
            for way, target in ((0, right), (1, left)):
                lane = way * CHUNKS + chunk
                rows = pl.ds(lane * (half // CHUNKS), half // CHUNKS)
                if step > 0:
                    sent[step - 1, lane].wait_recv()
                if step < n - 1:
                    source = x_ref.at[rows] if step == 0 else held.at[step - 1, rows]
                    copy = ring_copy(source, held.at[step, rows], sems, lane, step, target)
                    copy.start()
                    sent[step, lane] = copy
        if step == 0:
            for offset in order:
                w_copy(offset).start()
        for way in (0, 1):
            offset = (n - step) % n if way == 0 else step
            if offset not in loaded:
                w_copy(offset).wait()
                loaded.add(offset)
            where = columns(offset)
            rows = pl.ds(way * half, half)
            source = x_ref.at[rows] if step == 0 else held.at[step - 1, rows]

            def multiply(index, carry):
                outs = pl.ds(pl.multiple_of(index * tile, tile), tile)
                part = lax.dot_general(
                    source[...], w_ref[outs, where], LAST, preferred_element_type=jnp.float32
                )
                if step > 0:
                    part = part + total[rows, outs]
                if step < n - 1:
                    total[rows, outs] = part
                else:
                    o_ref[rows, outs] = part.astype(o_ref.dtype)
                return carry

            lax.fori_loop(0, width // tile, multiply, 0)
    for copy in sent.values():
        copy.wait_send()


def gather_matmul(x, w):
    n = lax.axis_size("head")
    tokens, depth = x.shape
    width = w.shape[0]
    vmem = pl.BlockSpec(memory_space=pltpu.VMEM)
    return pl.pallas_call(
        functools.partial(gather_matmul_kernel, n),
        out_shape=jax.ShapeDtypeStruct((tokens, width), jnp.bfloat16),
        in_specs=[vmem, pl.BlockSpec(memory_space=pltpu.HBM)],
        out_specs=vmem,
        scratch_shapes=[
            pltpu.VMEM((n - 1, tokens, depth), jnp.bfloat16),
            pltpu.VMEM(w.shape, jnp.bfloat16),
            pltpu.VMEM((tokens, width), jnp.float32),
            pltpu.SemaphoreType.DMA((2 * CHUNKS, n - 1)),
            pltpu.SemaphoreType.DMA((2 * CHUNKS, n - 1)),
            pltpu.SemaphoreType.DMA((n,)),
        ],
        compiler_params=pltpu.CompilerParams(
            collective_id=0, has_side_effects=True, vmem_limit_bytes=52 * 2**20
        ),
        name="gather_matmul",
    )(x, w)


def matmul_scatter_kernel(
    n, s, w_hbm, x_ref, bc_ref, p_ref, o_ref, obc_ref, op_ref,
    w_ref, going, coming, p_in, send_sem, recv_sem, w_sem, p_send, p_recv,
):
    me = lax.axis_index("head")
    mine = lax.axis_index("seq")
    right, left = (lax.rem(me + 1, n), lax.rem(me + n - 1, n))
    rows_here = o_ref.shape[0]
    half = rows_here // 2
    bc_half = obc_ref.shape[0] // 2
    piece = half // CHUNKS
    tile = tile_of(piece)

    def owner_of(way, step):
        return lax.rem(me + 2 * n - 1 - step, n) if way == 0 else lax.rem(me + 1 + step, n)

    def w_copy(way, step):
        start = pl.multiple_of(owner_of(way, step) * rows_here + way * half, half)
        rows = pl.ds(start, half)
        return pltpu.make_async_copy(w_hbm.at[rows], w_ref.at[rows], w_sem.at[way, step])

    for step in range(n):
        for way in (0, 1):
            w_copy(way, step).start()
    barrier = pltpu.get_barrier_semaphore()
    for neighbour in (left, right):
        pl.semaphore_signal(barrier, inc=1, device_id={"head": neighbour}, device_id_type=MESH)
    for away in range(1, s):
        pl.semaphore_signal(
            barrier, inc=1, device_id={"seq": lax.rem(mine + away, s)}, device_id_type=MESH
        )
    pl.semaphore_wait(barrier, 2 + s - 1)
    sems = (send_sem, recv_sem)
    p_copies = []
    for away in range(1, s):
        copy = pltpu.make_async_remote_copy(
            src_ref=p_ref,
            dst_ref=p_in.at[away - 1],
            send_sem=p_send.at[away - 1],
            recv_sem=p_recv.at[away - 1],
            device_id={"seq": lax.rem(mine + away, s)},
            device_id_type=MESH,
        )
        p_copies.append(copy)
    sent = {}
    for step in range(n):
        for chunk, way in ((c, w) for c in range(CHUNKS) for w in (0, 1)):
            target = left if way else right
            lane = way * CHUNKS + chunk
            owner = owner_of(way, step)
            if chunk == 0:
                w_copy(way, step).wait()
            if step > 0:
                sent[step - 1, lane].wait_recv()
            first = pl.multiple_of(owner * rows_here + way * half, half)

            def finish(start, count, part, target_ref, base):
                if step > 0:
                    old = coming[way, step - 1, pl.ds(start, count), :]
                    part = part.astype(jnp.bfloat16).astype(jnp.float32) + old.astype(jnp.float32)
                if step < n - 1:
                    going[way, step, pl.ds(start, count), :] = part.astype(jnp.bfloat16)
                else:
                    target_ref[pl.ds(base, count), :] = part.astype(jnp.bfloat16)

            def multiply(index, carry):
                start = pl.multiple_of(chunk * piece + index * tile, tile)
                part = lax.dot_general(
                    w_ref[pl.ds(first + start, tile), :],
                    x_ref[...],
                    LAST,
                    preferred_element_type=jnp.float32,
                )
                base = pl.multiple_of(way * half + start, tile)
                finish(start, tile, part, o_ref, base)
                return carry

            lax.fori_loop(0, piece // tile, multiply, 0)
            span = piece
            if chunk == CHUNKS - 1:
                span = piece + bc_half
                bc_start = pl.multiple_of(owner * 2 * bc_half + way * bc_half, bc_half)
                finish(half, bc_half, bc_ref[pl.ds(bc_start, bc_half), :], obc_ref, way * bc_half)
            if step < n - 1:
                rows = pl.ds(chunk * piece, span)
                copy = ring_copy(
                    going.at[way, step, rows], coming.at[way, step, rows], sems, lane, step, target
                )
                copy.start()
                sent[step, lane] = copy
        if step == 0:
            for copy in p_copies:
                copy.start()
    value = p_ref[...]
    for index, copy in enumerate(p_copies):
        copy.wait_recv()
        value = value + p_in[index]
    op_ref[...] = value
    for copy in p_copies + list(sent.values()):
        copy.wait_send()


def matmul_scatter(w, x, bc, params):
    n, s = (lax.axis_size("head"), lax.axis_size("seq"))
    tokens = x.shape[0]
    rows_here, bc_here = (w.shape[0] // n, bc.shape[0] // n)
    padded = jnp.zeros((8, 128), jnp.float32).at[: params.shape[0], : params.shape[1]].set(params)
    vmem = pl.BlockSpec(memory_space=pltpu.VMEM)
    packet = (2, n - 1, (rows_here + bc_here) // 2, tokens)
    in_sum, bc_sum, param_sum = pl.pallas_call(
        functools.partial(matmul_scatter_kernel, n, s),
        out_shape=(
            jax.ShapeDtypeStruct((rows_here, tokens), jnp.bfloat16),
            jax.ShapeDtypeStruct((bc_here, tokens), jnp.bfloat16),
            jax.ShapeDtypeStruct((8, 128), jnp.float32),
        ),
        in_specs=[pl.BlockSpec(memory_space=pltpu.HBM), vmem, vmem, vmem],
        out_specs=(vmem, vmem, vmem),
        scratch_shapes=[
            pltpu.VMEM(w.shape, jnp.bfloat16),
            pltpu.VMEM(packet, jnp.bfloat16),
            pltpu.VMEM(packet, jnp.bfloat16),
            pltpu.VMEM((s - 1, 8, 128), jnp.float32),
            pltpu.SemaphoreType.DMA((2 * CHUNKS, n - 1)),
            pltpu.SemaphoreType.DMA((2 * CHUNKS, n - 1)),
            pltpu.SemaphoreType.DMA((2, n)),
            pltpu.SemaphoreType.DMA((s - 1,)),
            pltpu.SemaphoreType.DMA((s - 1,)),
        ],
        compiler_params=pltpu.CompilerParams(
            collective_id=1, has_side_effects=True, vmem_limit_bytes=52 * 2**20
        ),
        name="matmul_scatter",
    )(w, x, bc, padded)
    return in_sum, bc_sum, param_sum[: params.shape[0], : params.shape[1]]


def shards(out_grad, x_in, b_in, c_in, dt_raw, dt_bias, a_log, d_skip, states, w_out, w_in):
    tokens_here, inner_here = x_in.shape
    group_heads = dt_raw.shape[0]
    head_dim = inner_here // group_heads
    state_dim = b_in.shape[1]
    contract_last = (((1,), (1,)), ((), ()))
    head_grad = gather_matmul(out_grad, w_out)
    dy_heads = head_grad.reshape(tokens_here, group_heads, head_dim)
    x_heads = x_in.reshape(tokens_here, group_heads, head_dim)
    x_wide = x_heads.astype(jnp.float32)
    decay_rate = jnp.exp(a_log)
    step_size = jax.nn.softplus(dt_raw + dt_bias[:, None])
    log_step = -decay_rate[:, None] * step_size
    cumlog = jnp.cumsum(log_step, axis=1)
    positions = jnp.arange(tokens_here)
    causal = positions[:, None] >= positions[None, :]
    log_gaps = cumlog[:, :, None] - cumlog[:, None, :]
    decay_mask = jnp.where(causal[None], jnp.exp(jnp.minimum(log_gaps, 0.0)), 0.0)
    start_decay = jnp.exp(cumlog)
    dy_decay = (dy_heads.astype(jnp.float32) * start_decay.T[:, :, None]).astype(jnp.bfloat16)
    local_state = jnp.einsum("ihp,in->hpn", dy_decay, c_in, preferred_element_type=jnp.float32)
    end_total = jnp.exp(cumlog[:, -1])
    carried, dy_heads = entering(end_total, local_state, "seq", dy_heads)
    dy_wide = dy_heads.astype(jnp.float32)
    scores = lax.dot_general(c_in, b_in, contract_last, preferred_element_type=jnp.float32)
    step_rows = step_size.T
    x_scaled = (x_wide * step_rows[:, :, None]).astype(jnp.bfloat16)
    pair_dots = jnp.einsum("ihp,jhp->hij", dy_heads, x_scaled, preferred_element_type=jnp.float32)
    kernel = (scores[None] * decay_mask).astype(jnp.bfloat16)
    intra_back = jnp.einsum("hij,ihp->jhp", kernel, dy_heads, preferred_element_type=jnp.float32)
    masked_dots = (pair_dots * decay_mask).astype(jnp.bfloat16)
    entry_state = states.reshape(group_heads, head_dim, state_dim)
    db_intra = jnp.einsum("hij,in->nj", masked_dots, c_in, preferred_element_type=jnp.float32)
    dc_intra = jnp.einsum("hij,jn->ni", masked_dots, b_in, preferred_element_type=jnp.float32)
    dc_entry = jnp.einsum("ihp,hpn->ni", dy_decay, entry_state, preferred_element_type=jnp.float32)
    ystate = jnp.einsum("in,hpn->ihp", c_in, entry_state, preferred_element_type=jnp.float32)
    pair_weight = pair_dots * scores[None] * decay_mask
    state_terms = start_decay * jnp.sum(dy_wide * ystate, axis=2).T
    skip_terms = jnp.sum(dy_wide * x_wide, axis=(0, 2))

    carried_bf = carried.astype(jnp.bfloat16)
    state_back = jnp.einsum("jn,hpn->jhp", b_in, carried_bf, preferred_element_type=jnp.float32)
    end_decay = jnp.exp(cumlog[:, -1:] - cumlog)
    end_weight = (step_size * end_decay).T
    x_grad = (
        (
            step_rows[:, :, None] * intra_back
            + end_weight[:, :, None] * state_back
            + d_skip[None, :, None] * dy_wide
        )
        .astype(jnp.bfloat16)
        .reshape(tokens_here, inner_here)
    )
    x_end = (x_wide * end_weight[:, :, None]).astype(jnp.bfloat16)
    db_entry = jnp.einsum("jhp,hpn->nj", x_end, carried_bf, preferred_element_type=jnp.float32)
    bc_part = jnp.concatenate([db_intra + db_entry, dc_intra + dc_entry], axis=0)
    end_terms = end_weight.T * jnp.sum(x_wide * state_back, axis=2).T
    cum_grad = pair_weight.sum(axis=2) - pair_weight.sum(axis=1) + state_terms - end_terms
    tail_grad = end_terms.sum(axis=1) + end_total * jnp.sum(
        entry_state.astype(jnp.float32) * carried, axis=(1, 2)
    )
    cum_grad = cum_grad.at[:, -1].add(tail_grad)
    step_grad = jnp.cumsum(cum_grad[:, ::-1], axis=1)[:, ::-1]
    dt_sum = (
        -decay_rate[:, None] * step_grad
        + jnp.sum(x_wide * (intra_back + end_decay.T[:, :, None] * state_back), axis=2).T
    )
    dt_grad = dt_sum * jax.nn.sigmoid(dt_raw + dt_bias[:, None])
    param_terms = jnp.stack(
        [jnp.sum(step_grad * log_step, axis=1), skip_terms, jnp.sum(dt_grad, axis=1)]
    )
    in_part, bc_sum, param_sum = matmul_scatter(w_in, x_grad, bc_part, param_terms)
    norm_scale = (lax.axis_size("seq") * tokens_here * head_dim) ** (-0.5)
    param_grad = param_sum * norm_scale
    return (in_part, bc_sum, dt_grad, param_grad)


def solution(mesh):
    return jax.shard_map(
        shards,
        mesh=mesh,
        in_specs=(
            P("seq", "head"),
            P("seq", "head"),
            P("seq", None),
            P("seq", None),
            P("head", "seq"),
            P("head"),
            P("head"),
            P("head"),
            P("seq", "head", None),
            P("head", None),
            P(None, "head"),
        ),
        out_specs=(P("head", "seq"), P("head", "seq"), P("head", "seq"), P(None, "head")),
        check_vma=False,
    )
```
